32 devices in a mesh: band: 16 (over z, y, x), head: 2 (over core).
Axes of the slice: x: 2, y: 2, z: 4, core: 2. Of those that a mesh axis runs over, the one named last changes fastest.
Arguments:
- image_in: bfloat16 [1024, 8, 1024], P('band'), may hold values from -6 to 6
- text_states: bfloat16 [512, 1024], P('band'), may hold values from -6 to 6
- norm_gains: float32 [3, 1024], replicated, may hold values from 0.1 to 1.9
- norm_biases: float32 [3, 1024], replicated, may hold values from -2 to 2
- w_qkv: bfloat16 [1024, 3, 1024], P(None, None, 'head'), may hold values from -0.1875 to 0.1875
- w_out: bfloat16 [1024, 1024], P('head'), may hold values from -0.75 to 0.75
- w_cq: bfloat16 [1024, 1024], P(None, 'head'), may hold values from -0.1875 to 0.1875
- w_ckv: bfloat16 [1024, 2, 1024], P(None, None, 'head'), may hold values from -0.1875 to 0.1875
- w_co: bfloat16 [1024, 1024], P('head'), may hold values from -0.375 to 0.375
- w_up: bfloat16 [1024, 4096], P(None, 'head'), may hold values from -0.1875 to 0.1875
- w_down: bfloat16 [4096, 1024], P('head'), may hold values from -0.09375 to 0.09375
- seg_ids: int32 [512], replicated, may hold values from 0 to 7, never falling along the last dimension, each value on 1 to 128 neighbouring positions
- image_seg: int32 [8], replicated, may hold values from 0 to 7, each once
- out_cotangent: bfloat16 [1024, 8, 1024], P('band'), may hold values from -6 to 6
Outputs:
- block_out: bfloat16 [1024, 8, 1024], P('band')
- grad_image_in: float32 [1024, 8, 1024], P('band')
- grad_text_states: float32 [512, 1024], P('band')
- grad_norm_gains: float32 [3, 1024], P(None, 'band')
- grad_norm_biases: float32 [3, 1024], P(None, 'band')
- grad_w_qkv: float32 [1024, 3, 1024], P('band', None, 'head')
- grad_w_out: float32 [1024, 1024], P('head', 'band')
- grad_w_cq: float32 [1024, 1024], P('band', 'head')
- grad_w_ckv: float32 [1024, 2, 1024], P('band', None, 'head')
- grad_w_co: float32 [1024, 1024], P('head', 'band')
- grad_w_up: float32 [1024, 4096], P('band', 'head')
- grad_w_down: float32 [4096, 1024], P('head', 'band')
The draws below stay inside these ranges and needn't reach their ends.
Inputs may be any that keep to these rules, and one draw needn't show every extreme that they name: `seg_ids`: the 8 captions, of 1 to 128 tokens each, are packed end to end: caption numbers never fall along the text tokens, every caption is one run, and some caption has exactly 128 tokens. `image_seg`: each image names a different caption.
All inputs are finite; a program needn't handle non-finite values.
Results may differ from the reference program's by a relative error of at most 0.025.
Values may be sent and summed in bfloat16 or wider, within the bound.
No kernel may reach another device: no remote copies, remote signals or barrier semaphores. Data moves between devices by JAX's collectives and lax.ppermute only.
A program may use at most 256 MiB of HBM per device.

```python
import math
import jax
import jax.numpy as jnp
import numpy as np
from jax import lax

D = 1024
HEADS = 16
HD = 64
FF = 4096
POS = 1024
ENC_LEN = 128
IMAGES = 8
TEXT_TOK = 512


def shard_levels(key, dims, shards, low, high):
    level, own = 1.0, jax.random.fold_in(key, 6)
    for axis_at, blocks in shards:
        draws = jnp.exp(jax.random.uniform(jax.random.fold_in(own, axis_at), (blocks,), jnp.float32, low / len(shards), high / len(shards)))
        level = level * jnp.repeat(draws, dims[axis_at] // blocks).reshape([-1 if axis == axis_at else 1 for axis in range(len(dims))])
    return level


def split_up(number_of, total, reach, slope):
    weights = [(1 << 20) // math.isqrt(standing ** slope) + 1 for standing in range(2, number_of + 1)]
    spare, counts = total - reach - (number_of - 1), [1] * (number_of - 1)
    while spare > 0:
        free = [i for i in range(number_of - 1) if counts[i] < reach]
        whole, remaining = sum([weights[i] for i in free]), spare
        for i in free:
            addition = min(reach - counts[i], max(1, remaining * weights[i] // whole), spare)
            counts[i] = counts[i] + addition
            spare = spare - addition
    return np.array([reach] + counts)


def ragged_sizes(rng, amount, total, bound, slope):
    if amount == 2:
        one = jax.random.randint(rng, (), max(1, total - bound), min(bound, total - 1) + 1)
        return jnp.stack([one, total - one])
    tallies = jnp.asarray(split_up(amount, total, bound, slope), jnp.int32)
    pairs = (amount - 1) // 2
    donor, taker = tallies[1:1 + 2 * pairs:2], tallies[2:2 + 2 * pairs:2]
    slack = jnp.minimum(donor - 1, bound - taker)
    shifted = jax.random.randint(jax.random.fold_in(rng, 1), (pairs,), 0, 1 << 20) % (slack + 1)
    tallies = tallies.at[1:1 + 2 * pairs:2].set(donor - shifted).at[2:2 + 2 * pairs:2].set(taker + shifted)
    return tallies[jax.random.permutation(jax.random.fold_in(rng, 2), amount)]


def bell_draw(stream_key, extent, deviation, limit, shards=(), dtype=jnp.bfloat16):
    loudness = shard_levels(stream_key, extent, shards, -0.22, 0.18) if shards else 1.0
    entries = jax.random.normal(stream_key, extent, jnp.float32) * deviation * loudness
    return jnp.minimum(jnp.maximum(entries, -limit), limit).astype(dtype)


def setup_inputs(seed: int = 0) -> dict:
    arg_keys = jax.random.split(jax.random.key(seed), 15)
    return {
        "image_in": bell_draw(arg_keys[0], (POS, IMAGES, D), 1.0, 6.0, ((0, 16),)),
        "text_states": bell_draw(arg_keys[1], (TEXT_TOK, D), 1.0, 6.0, ((0, 16),)),
        "norm_gains": jnp.clip(1.0 + 0.18 * jax.random.normal(arg_keys[2], (3, D), jnp.float32), 0.1, 1.9),
        "norm_biases": bell_draw(arg_keys[3], (3, D), 0.3, 2.0, (), jnp.float32),
        "w_qkv": bell_draw(arg_keys[4], (D, 3, HEADS * HD), D ** -0.5, 0.1875, ((2, 2),)),
        "w_out": bell_draw(arg_keys[5], (HEADS * HD, D), (D // 16) ** -0.5, 0.75, ((0, 2),)),
        "w_cq": bell_draw(arg_keys[6], (D, HEADS * HD), D ** -0.5, 0.1875, ((1, 2),)),
        "w_ckv": bell_draw(arg_keys[7], (D, 2, HEADS * HD), D ** -0.5, 0.1875, ((2, 2),)),
        "w_co": bell_draw(arg_keys[8], (HEADS * HD, D), (D // 4) ** -0.5, 0.375, ((0, 2),)),
        "w_up": bell_draw(arg_keys[9], (D, FF), D ** -0.5, 0.1875, ((1, 2),)),
        "w_down": bell_draw(arg_keys[10], (FF, D), FF ** -0.5, 0.09375, ((0, 2),)),
        "seg_ids": jnp.searchsorted(jnp.cumsum(ragged_sizes(arg_keys[11], IMAGES, TEXT_TOK, ENC_LEN, 1)), jnp.arange(TEXT_TOK), side="right").astype(jnp.int32),
        "image_seg": jax.random.permutation(arg_keys[12], IMAGES).astype(jnp.int32),
        "out_cotangent": bell_draw(arg_keys[13], (POS, IMAGES, D), 1.0, 6.0, ((0, 16),)),
    }


@jax.custom_vjp
def low(v):
    return lax.optimization_barrier(v.astype(jnp.bfloat16)).astype(jnp.float32)

@jax.custom_vjp
def low_back(v):
    return v

def low_keep(v):
    return (low(v), None)

def low_pass(kept, grad):
    return (grad,)

def back_keep(v):
    return (v, None)

def back_low(kept, grad):
    return (low(grad),)
low.defvjp(low_keep, low_pass)
low_back.defvjp(back_keep, back_low)
NEG_BIG = -1e+30

def normalize(values, gain_row, bias_row):
    row_mean = lax.optimization_barrier(jnp.mean(values, axis=-1, keepdims=True))
    centered = values - row_mean
    variance = lax.optimization_barrier(jnp.mean(centered * centered, axis=-1, keepdims=True))
    return centered * lax.rsqrt(variance + 1e-05) * gain_row + bias_row

def matmul(left_side, right_side):
    return jnp.dot(left_side, right_side, precision=lax.Precision.HIGHEST)

def product(einsum_form, left_side, right_side):
    return jnp.einsum(einsum_form, left_side, right_side, precision=lax.Precision.HIGHEST)

def reference(image_in, text_states, norm_gains, norm_biases, w_qkv, w_out, w_cq, w_ckv, w_co, w_up, w_down, seg_ids, image_seg, out_cotangent):
    head_cols = HEADS * HD
    score_scale = HD ** (-0.5)
    positions = jnp.arange(POS)
    causal = positions[None, :] <= positions[:, None]

    def forward(image_arg, text_arg, gain_arg, bias_arg, qkv_weight, out_weight, cq_weight, ckv_weight, co_weight, up_weight, down_weight):
        text_kv = low_back(low(matmul(text_arg, ckv_weight.reshape(D, 2 * head_cols))))
        text_kv = text_kv.reshape(TEXT_TOK, 2, HEADS, HD)

        def one_image(image_pair):
            image_rows, caption = image_pair
            normed1 = low(normalize(image_rows, gain_arg[0], bias_arg[0]))
            qkv_rows = low_back(low(matmul(normed1, qkv_weight.reshape(D, 3 * head_cols))))
            qkv_rows = qkv_rows.reshape(POS, 3, HEADS, HD)
            scores = low_back(product('phd,khd->hpk', qkv_rows[:, 0], qkv_rows[:, 1]) * score_scale)
            scores = jnp.where(causal[None], scores, NEG_BIG)
            self_prob = low(jax.nn.softmax(scores, axis=-1))
            attended = product('hpk,khd->phd', self_prob, qkv_rows[:, 2]).reshape(POS, head_cols)
            attended = low_back(low(attended))
            stream1 = image_rows + low_back(matmul(attended, out_weight))
            normed2 = low(normalize(stream1, gain_arg[1], bias_arg[1]))
            cross_q = low_back(low(matmul(normed2, cq_weight))).reshape(POS, HEADS, HD)
            cross_scores = low_back(product('phd,thd->hpt', cross_q, text_kv[:, 0]) * score_scale)
            own_caption = (seg_ids == caption)[None, None, :]
            cross_scores = jnp.where(own_caption, cross_scores, NEG_BIG)
            cross_prob = low(jax.nn.softmax(cross_scores, axis=-1))
            cross_att = product('hpt,thd->phd', cross_prob, text_kv[:, 1]).reshape(POS, head_cols)
            cross_att = low_back(low(cross_att))
            stream2 = stream1 + low_back(matmul(cross_att, co_weight))
            normed3 = low(normalize(stream2, gain_arg[2], bias_arg[2]))
            up_proj = low_back(matmul(normed3, up_weight))
            hidden = low(jax.nn.gelu(up_proj, approximate=True))
            return stream2 + matmul(hidden, down_weight)
        image_outs = lax.map(jax.checkpoint(one_image), (jnp.moveaxis(image_arg, 1, 0), image_seg))
        return jnp.moveaxis(image_outs, 0, 1)
    single = jnp.float32
    block_out, pullback = jax.vjp(forward, image_in.astype(single), text_states.astype(single), norm_gains, norm_biases, w_qkv.astype(single), w_out.astype(single), w_cq.astype(single), w_ckv.astype(single), w_co.astype(single), w_up.astype(single), w_down.astype(single))
    gradients = pullback(out_cotangent.astype(single))
    return (block_out.astype(jnp.bfloat16), gradients[0], gradients[1], gradients[2], gradients[3], gradients[4], gradients[5], gradients[6], gradients[7], gradients[8], gradients[9], gradients[10])
```

```python
from functools import partial

import jax
import jax.numpy as jnp
from jax import lax
from jax.experimental import pallas as pl
from jax.experimental.pallas import tpu as pltpu
from jax.sharding import PartitionSpec as P

HD = 64
NEG_BIG = -1e30
SCALE = HD ** (-0.5)
BF = jnp.bfloat16
F32 = jnp.float32


def normalize(values, gain_row, bias_row):
    row_mean = jnp.mean(values, axis=-1, keepdims=True)
    centered = values - row_mean
    variance = jnp.mean(centered * centered, axis=-1, keepdims=True)
    return centered * lax.rsqrt(variance + 1e-05) * gain_row + bias_row


def norm_back(values, gain_row, grad_n):
    row_mean = jnp.mean(values, axis=-1, keepdims=True)
    centered = values - row_mean
    variance = jnp.mean(centered * centered, axis=-1, keepdims=True)
    rstd = lax.rsqrt(variance + 1e-05)
    xhat = centered * rstd
    scaled = grad_n * gain_row
    mean_e = jnp.mean(scaled, axis=-1, keepdims=True)
    mean_ex = jnp.mean(scaled * xhat, axis=-1, keepdims=True)
    grad_v = rstd * (scaled - mean_e - xhat * mean_ex)
    return grad_v, jnp.sum(grad_n * xhat, axis=0), jnp.sum(grad_n, axis=0)


def norm_terms(values, grad_n):
    row_mean = jnp.mean(values, axis=-1, keepdims=True)
    centered = values - row_mean
    variance = jnp.mean(centered * centered, axis=-1, keepdims=True)
    xhat = centered * lax.rsqrt(variance + 1e-05)
    return jnp.sum(grad_n * xhat, axis=0), jnp.sum(grad_n, axis=0)


def dot(left, right, contract):
    return lax.dot_general(left, right, (contract, ((), ())), preferred_element_type=F32)


def matmul(left, right):
    return dot(left, right, ((1,), (0,)))


def mat_left_t(left, right):
    return dot(left, right, ((0,), (0,)))


def mat_right_t(left, right):
    return dot(left, right, ((1,), (1,)))


def self_fwd_kernel(q_ref, k_ref, v_ref, o_ref, *, blk):
    rows, width = q_ref.shape
    keep = lax.broadcasted_iota(jnp.int32, (blk, blk), 1) <= lax.broadcasted_iota(
        jnp.int32, (blk, blk), 0
    )
    for h in range(width // HD):
        c = slice(h * HD, (h + 1) * HD)
        for j in range(rows // blk):
            lo = j * blk
            own = slice(lo, lo + blk)
            q = q_ref[own, c] * SCALE
            s = jnp.where(keep, mat_right_t(q, k_ref[own, c]), NEG_BIG)
            m = jnp.max(s, axis=1, keepdims=True)
            if j:
                so = mat_right_t(q, k_ref[:lo, c])
                m = jnp.maximum(m, jnp.max(so, axis=1, keepdims=True))
            e = jnp.exp(s - m)
            total = jnp.sum(e, axis=1, keepdims=True)
            acc = matmul(e.astype(BF), v_ref[own, c])
            if j:
                eo = jnp.exp(so - m)
                total = total + jnp.sum(eo, axis=1, keepdims=True)
                acc = acc + matmul(eo.astype(BF), v_ref[:lo, c])
            o_ref[own, c] = (acc / total).astype(BF)


def self_bwd_kernel(q_ref, k_ref, v_ref, g_ref, dq_ref, dk_ref, dv_ref, ak_ref, av_ref, *, blk):
    rows, width = q_ref.shape
    keep = lax.broadcasted_iota(jnp.int32, (blk, blk), 0) <= lax.broadcasted_iota(
        jnp.int32, (blk, blk), 1
    )
    for h in range(width // HD):
        c = slice(h * HD, (h + 1) * HD)
        for j in reversed(range(rows // blk)):
            lo = j * blk
            own = slice(lo, lo + blk)
            q = q_ref[own, c] * SCALE
            g = g_ref[own, c]
            kd, vd = k_ref[own, c], v_ref[own, c]
            s = jnp.where(keep, mat_right_t(kd, q), NEG_BIG)
            m = jnp.max(s, axis=0, keepdims=True)
            if j:
                ko, vo = k_ref[:lo, c], v_ref[:lo, c]
                so = mat_right_t(ko, q)
                m = jnp.maximum(m, jnp.max(so, axis=0, keepdims=True))
            e = jnp.exp(s - m)
            total = jnp.sum(e, axis=0, keepdims=True)
            if j:
                eo = jnp.exp(so - m)
                total = total + jnp.sum(eo, axis=0, keepdims=True)
            inv = 1.0 / total
            p = e * inv
            dp = mat_right_t(vd, g)
            row = jnp.sum(p * dp, axis=0, keepdims=True)
            if j:
                po = eo * inv
                dpo = mat_right_t(vo, g)
                row = row + jnp.sum(po * dpo, axis=0, keepdims=True)
            ds = (p * (dp - row)).astype(BF)
            dq = mat_left_t(ds, kd)
            dk = matmul(ds, q)
            dv = matmul(p.astype(BF), g)
            last = lo + blk == rows
            if last:
                ak_ref[own, c] = dk
                av_ref[own, c] = dv
            else:
                ak_ref[own, c] += dk
                av_ref[own, c] += dv
            if j:
                dso = (po * (dpo - row)).astype(BF)
                dq = dq + mat_left_t(dso, ko)
                dko = matmul(dso, q)
                dvo = matmul(po.astype(BF), g)
                if last:
                    ak_ref[:lo, c] = dko
                    av_ref[:lo, c] = dvo
                else:
                    ak_ref[:lo, c] += dko
                    av_ref[:lo, c] += dvo
            dq_ref[own, c] = (dq * SCALE).astype(BF)
    dk_ref[...] = ak_ref[...].astype(BF)
    dv_ref[...] = av_ref[...].astype(BF)


def cross_fwd_kernel(q_ref, k_ref, v_ref, img_ref, seg_ref, o_ref, *, blk):
    rows, width = q_ref.shape
    for h in range(width // HD):
        c = slice(h * HD, (h + 1) * HD)
        for j in range(rows // blk):
            own = slice(j * blk, (j + 1) * blk)
            q = q_ref[own, c] * SCALE
            s = jnp.where(img_ref[own] == seg_ref[...], mat_right_t(q, k_ref[:, c]), NEG_BIG)
            e = jnp.exp(s - jnp.max(s, axis=1, keepdims=True))
            total = jnp.sum(e, axis=1, keepdims=True)
            o_ref[own, c] = (matmul(e.astype(BF), v_ref[:, c]) / total).astype(BF)


def cross_bwd_kernel(q_ref, k_ref, v_ref, g_ref, img_ref, seg_ref, dq_ref, dk_ref, dv_ref, *, blk):
    rows, width = q_ref.shape
    for h in range(width // HD):
        c = slice(h * HD, (h + 1) * HD)
        k, v = k_ref[:, c], v_ref[:, c]
        dk = dv = None
        for j in range(rows // blk):
            own = slice(j * blk, (j + 1) * blk)
            q = q_ref[own, c] * SCALE
            g = g_ref[own, c]
            s = jnp.where(seg_ref[...] == img_ref[:, own], mat_right_t(k, q), NEG_BIG)
            e = jnp.exp(s - jnp.max(s, axis=0, keepdims=True))
            p = e * (1.0 / jnp.sum(e, axis=0, keepdims=True))
            dp = mat_right_t(v, g)
            ds = (p * (dp - jnp.sum(p * dp, axis=0, keepdims=True))).astype(BF)
            dq_ref[own, c] = (mat_left_t(ds, k) * SCALE).astype(BF)
            a, b = matmul(ds, q), matmul(p.astype(BF), g)
            dk, dv = (a, b) if dk is None else (dk + a, dv + b)
        dk_ref[:, c] = dk.astype(BF)
        dv_ref[:, c] = dv.astype(BF)


def cols_spec(rows, width):
    return pl.BlockSpec((rows, width), lambda i: (0, i))


def whole_spec(shape):
    return pl.BlockSpec(shape, lambda i: (0, 0))


def self_attention(q, k, v):
    rows, cols = q.shape
    width = min(128, cols)
    spec = cols_spec(rows, width)
    return pl.pallas_call(
        partial(self_fwd_kernel, blk=256),
        grid=(cols // width,),
        in_specs=[spec] * 3,
        out_specs=spec,
        out_shape=jax.ShapeDtypeStruct((rows, cols), BF),
        name="self_fwd",
    )(q, k, v)


def self_attention_back(q, k, v, g):
    rows, cols = q.shape
    width = min(128, cols)
    spec = cols_spec(rows, width)
    return pl.pallas_call(
        partial(self_bwd_kernel, blk=256),
        grid=(cols // width,),
        in_specs=[spec] * 4,
        out_specs=[spec] * 3,
        out_shape=[jax.ShapeDtypeStruct((rows, cols), BF)] * 3,
        scratch_shapes=[pltpu.VMEM((rows, width), F32)] * 2,
        name="self_bwd",
    )(q, k, v, g)


def cross_attention(q, k, v, img, seg):
    rows, cols = q.shape
    keys = k.shape[0]
    width = min(128, cols)
    return pl.pallas_call(
        partial(cross_fwd_kernel, blk=256),
        grid=(cols // width,),
        in_specs=[
            cols_spec(rows, width),
            cols_spec(keys, width),
            cols_spec(keys, width),
            whole_spec((rows, 1)),
            whole_spec((1, keys)),
        ],
        out_specs=cols_spec(rows, width),
        out_shape=jax.ShapeDtypeStruct((rows, cols), BF),
        name="cross_fwd",
    )(q, k, v, img[:, None], seg[None, :])


def cross_attention_back(q, k, v, g, img, seg):
    rows, cols = q.shape
    keys = k.shape[0]
    width = min(128, cols)
    return pl.pallas_call(
        partial(cross_bwd_kernel, blk=256),
        grid=(cols // width,),
        in_specs=[
            cols_spec(rows, width),
            cols_spec(keys, width),
            cols_spec(keys, width),
            cols_spec(rows, width),
            whole_spec((1, rows)),
            whole_spec((keys, 1)),
        ],
        out_specs=[cols_spec(rows, width), cols_spec(keys, width), cols_spec(keys, width)],
        out_shape=[
            jax.ShapeDtypeStruct((rows, cols), BF),
            jax.ShapeDtypeStruct((keys, cols), BF),
            jax.ShapeDtypeStruct((keys, cols), BF),
        ],
        name="cross_bwd",
    )(q, k, v, g, img[None, :], seg[:, None])


def head_swap(value):
    return lax.ppermute(value, "head", [(0, 1), (1, 0)])


def band_flip(value, bit, bands):
    return lax.ppermute(value, "band", [(i, i ^ (1 << bit)) for i in range(bands)])


def pick(array, axis, index):
    return lax.dynamic_index_in_dim(array, index, axis, keepdims=False)


def scatter_bits(mats, order, bands, band):
    bits = bands.bit_length() - 1
    left = list(range(bits))[::-1]
    parts = [m.reshape((2,) * bits + (m.shape[0] // bands, m.shape[1])) for m in mats]
    for bit in order:
        axis = left.index(bit)
        left.remove(bit)
        own = (band >> bit) & 1
        send = jnp.concatenate([pick(p, axis, 1 - own) for p in parts], axis=-1)
        keep = jnp.concatenate([pick(p, axis, own) for p in parts], axis=-1)
        got = band_flip(send, bit, bands)
        parts = [(keep.astype(F32) + got.astype(F32)).astype(BF)]
    out = parts[0]
    return out.reshape((-1,) + out.shape[-2:])


def body(
    image_in,
    text_states,
    norm_gains,
    norm_biases,
    w_qkv,
    w_out,
    w_cq,
    w_ckv,
    w_co,
    w_up,
    w_down,
    seg_ids,
    image_seg,
    out_cotangent,
    *,
    bands,
    heads,
):
    pos_dev, images, features = image_in.shape
    rows = pos_dev * images
    cols = w_qkv.shape[2]
    halves = bands // images
    own_cols = cols // halves
    positions = pos_dev * bands
    sub = pos_dev // heads
    band = lax.axis_index("band")
    head = lax.axis_index("head")
    half = band % halves
    gelu_tanh = partial(jax.nn.gelu, approximate=True)

    def head_sum(value):
        return value + head_swap(value) if heads == 2 else lax.psum(value, "head")

    def head_gather(value):
        if heads == 2:
            other = head_swap(value)
            return jnp.stack(
                [jnp.where(head == 0, value, other), jnp.where(head == 0, other, value)], axis=1
            )
        return lax.all_gather(value, "head", axis=1)

    def head_scatter(value):
        if heads == 2:
            return pick(value, 1, head).astype(F32) + head_swap(pick(value, 1, 1 - head)).astype(F32)
        return lax.psum_scatter(value, "head", scatter_dimension=1, tiled=False).astype(F32)

    x_rows = jnp.swapaxes(image_in, 0, 1)
    mine = lax.dynamic_slice_in_dim(x_rows, head * sub, sub, axis=1)
    sent = jnp.broadcast_to(mine[:, None], (images, halves, sub, features))
    got = lax.all_to_all(sent.reshape(bands * sub, features), "band", 0, 0, tiled=True)
    img_rows = head_gather(got.reshape(bands, sub, features)).reshape(positions, features)
    img_rows = img_rows.astype(F32)
    all_text = lax.all_gather(text_states, "band", axis=0, tiled=True)

    normed1 = normalize(img_rows, norm_gains[0], norm_biases[0]).astype(BF)
    w_own = lax.dynamic_slice_in_dim(w_qkv, half * own_cols, own_cols, axis=2)
    queries = matmul(normed1, w_own[:, 0]).astype(BF)
    keys = matmul(normed1, w_own[:, 1]).astype(BF)
    values = matmul(normed1, w_own[:, 2]).astype(BF)
    own_att = self_attention(queries, keys, values)
    self_att = lax.all_to_all(own_att, "band", 0, 0, tiled=True)
    self_att = self_att.reshape(images, halves, pos_dev, own_cols)
    self_att = jnp.swapaxes(self_att, 1, 2).reshape(rows, cols)

    stream = x_rows.astype(F32).reshape(rows, features)
    stream1 = stream + head_sum(matmul(self_att, w_out))
    normed2 = normalize(stream1, norm_gains[1], norm_biases[1]).astype(BF)
    cross_q = matmul(normed2, w_cq).astype(BF)
    w_tk, w_tv = w_ckv[:, 0], w_ckv[:, 1]
    text_k = matmul(all_text, w_tk).astype(BF)
    text_v = matmul(all_text, w_tv).astype(BF)
    row_seg = jnp.repeat(image_seg, pos_dev)
    cross_att = cross_attention(cross_q, text_k, text_v, row_seg, seg_ids)
    stream2 = stream1 + head_sum(matmul(cross_att, w_co))
    normed3 = normalize(stream2, norm_gains[2], norm_biases[2]).astype(BF)
    up_proj = matmul(normed3, w_up)
    hidden, gelu_pull = jax.vjp(gelu_tanh, up_proj)
    hidden = hidden.astype(BF)

    grad_rows = jnp.swapaxes(out_cotangent, 0, 1).reshape(rows, features)
    grad_hidden = mat_right_t(grad_rows, w_down)
    grad_up = gelu_pull(grad_hidden)[0].astype(BF)
    grad_n3 = head_sum(mat_right_t(grad_up, w_up))
    grad_down_t = mat_left_t(grad_rows, hidden).astype(BF)
    sum_down = scatter_bits([grad_down_t], (0, 1, 2, 3), bands, band)
    grad_w_up = mat_left_t(normed3, grad_up).astype(BF)
    sum_up = scatter_bits([grad_w_up], (1, 2, 0, 3), bands, band)
    stream3 = stream2 + head_sum(matmul(hidden, w_down).astype(BF)).astype(F32)
    block_out = jnp.swapaxes(stream3.astype(BF).reshape(images, pos_dev, features), 0, 1)

    back3, gain3, bias3 = norm_back(stream2, norm_gains[2], grad_n3)
    grad_stream2 = grad_rows.astype(F32) + back3
    grad_cross_out = grad_stream2.astype(BF)
    grad_co_t = mat_left_t(grad_cross_out, cross_att).astype(BF)
    grad_cross_att = mat_right_t(grad_cross_out, w_co).astype(BF)
    grad_cross_q, grad_tk, grad_tv = cross_attention_back(
        cross_q, text_k, text_v, grad_cross_att, row_seg, seg_ids
    )
    grad_n2 = head_sum(mat_right_t(grad_cross_q, w_cq))
    grad_w_cq = mat_left_t(normed2, grad_cross_q).astype(BF)
    grad_w_tk = mat_left_t(all_text, grad_tk).astype(BF)
    grad_w_tv = mat_left_t(all_text, grad_tv).astype(BF)
    text_grads = lax.psum_scatter(
        jnp.concatenate([grad_tk, grad_tv], axis=1), "band", scatter_dimension=0, tiled=True
    )
    grad_text_states = head_sum(
        mat_right_t(text_grads[:, :cols], w_tk) + mat_right_t(text_grads[:, cols:], w_tv)
    )

    back2, gain2, bias2 = norm_back(stream1, norm_gains[1], grad_n2)
    grad_stream1 = grad_stream2 + back2
    grad_self_out = grad_stream1.astype(BF)
    grad_out_t = mat_left_t(grad_self_out, self_att).astype(BF)
    grad_att = mat_right_t(grad_self_out, w_out).astype(BF)
    grad_att = jnp.swapaxes(grad_att.reshape(images, pos_dev, halves, own_cols), 1, 2)
    own_grad = lax.all_to_all(grad_att.reshape(positions, own_cols), "band", 0, 0, tiled=True)
    sum_mid = scatter_bits(
        [grad_co_t, grad_w_cq, grad_w_tk, grad_w_tv, grad_out_t], (2, 0, 1, 3), bands, band
    )

    grad_qkv = self_attention_back(queries, keys, values, own_grad)
    grad_qkv = jnp.concatenate(grad_qkv, axis=1)
    w_own = w_own.reshape(features, 3 * own_cols)
    part_n1 = mat_right_t(grad_qkv, w_own)
    block = part_n1.astype(BF).reshape(bands, heads, sub, features)
    block = head_scatter(block).astype(BF).reshape(bands // 2, 2, sub, features)
    low_bit = band & 1
    block = pick(block, 1, low_bit).astype(F32) + band_flip(
        pick(block, 1, 1 - low_bit), 0, bands
    ).astype(F32)
    groups = [[2 * i + b for i in range(bands // 2)] for b in range(2)]
    block = lax.all_to_all(
        block.astype(BF).reshape(images * sub, features),
        "band",
        0,
        0,
        axis_index_groups=groups,
        tiled=True,
    )
    grad_n1 = head_gather(block.reshape(images, sub, features)).reshape(rows, features)
    back1 = norm_back(stream, norm_gains[0], grad_n1.astype(F32))[0]
    grad_image = (grad_stream1 + back1).reshape(images, pos_dev, features)
    grad_image = jnp.swapaxes(grad_image, 0, 1)

    grad_w_qkv = mat_left_t(normed1, grad_qkv).astype(BF)
    terms1 = head_sum(jnp.stack(norm_terms(img_rows, part_n1)))
    terms = jnp.stack([terms1, jnp.stack([gain2, bias2]), jnp.stack([gain3, bias3])])
    chunk = features // bands
    terms = terms.astype(BF).reshape(3, 2, bands, chunk).transpose(2, 0, 1, 3)
    terms = terms.reshape(bands, 3, 2 * chunk)
    terms = jnp.pad(terms, ((0, 0), (0, chunk - 3), (0, 0))).reshape(features, 2 * chunk)
    last = scatter_bits([grad_w_qkv, terms], (1, 2, 3), bands, band)
    kept = pick(last, 0, low_bit)
    came = band_flip(pick(last, 0, 1 - low_bit), 0, bands)
    summed = (kept[:3, 3 * own_cols :].astype(F32) + came[:3, 3 * own_cols :].astype(F32)).reshape(
        3, 2, chunk
    )
    kept, came = (
        a[:, : 3 * own_cols].astype(F32).reshape(chunk, 3, own_cols) for a in (kept, came)
    )
    sum_qkv = jnp.where(
        half == 0, jnp.concatenate([kept, came], axis=2), jnp.concatenate([came, kept], axis=2)
    )
    mid = sum_mid[0].astype(F32)
    sum_co, sum_cq, sum_tk, sum_tv, sum_out = (
        mid[:, i * cols : (i + 1) * cols] for i in range(5)
    )
    return (
        block_out,
        grad_image,
        grad_text_states,
        summed[:, 0],
        summed[:, 1],
        sum_qkv,
        sum_out.T,
        sum_cq,
        jnp.stack([sum_tk, sum_tv], axis=1),
        sum_co.T,
        sum_up[0].astype(F32),
        sum_down[0].astype(F32).T,
    )


def solution(mesh):
    placed = (
        P("band", None, None),
        P("band", None),
        P(),
        P(),
        P(None, None, "head"),
        P("head", None),
        P(None, "head"),
        P(None, None, "head"),
        P("head", None),
        P(None, "head"),
        P("head", None),
        P(),
        P(),
        P("band", None, None),
    )
    return jax.shard_map(
        partial(body, bands=mesh.shape["band"], heads=mesh.shape["head"]),
        mesh=mesh,
        in_specs=placed,
        out_specs=(
            P("band", None, None),
            P("band", None, None),
            P("band", None),
            P(None, "band"),
            P(None, "band"),
            P("band", None, "head"),
            P("head", "band"),
            P("band", "head"),
            P("band", None, "head"),
            P("head", "band"),
            P("band", "head"),
            P("head", "band"),
        ),
        check_vma=False,
    )
```
